32 devices in a mesh: grp: 2 (over y), node: 4 (over z), sub: 2 (over x), rep: 2 (over core).
Axes of the slice: x: 2, y: 2, z: 4, core: 2. Of those that a mesh axis runs over, the one named last changes fastest.
Arguments:
- meson_nodes: float32 [2, 16, 512, 512], P(None, ('grp', 'node'), 'sub', 'rep'), parts along dimension 1, may hold values from -0.66 to 0.66
- term_nodes: int32 [8, 2], P('grp'), parts along dimension 0, may hold values from 0 to 7, as said below
- weight_codes: int32 [8], P('grp'), parts along dimension 0, may hold values from 0 to 7
- resident_pick: int32 [16], P('grp'), parts along dimension 0, may hold values from 0 to 1
Outputs:
- contracted: float32 [2, 16, 512, 512], P(None, ('grp', 'node'), 'sub', 'rep'), parts along dimension 1
The draws below stay inside these ranges and needn't reach their ends.
There are 2 independent parts, one for each index of `grp`. The reference program is written for one: setup_inputs(seed, part) draws one part's arguments, and reference() takes and returns one part's arrays. A program takes and returns all parts, laid end to end along the dimension named above; each array names one. Nothing has to cross between parts.
Inputs may be any that keep to these rules, and one draw needn't show every extreme that they name: `term_nodes`: node n belongs to owner n // 2. In every term the two nodes differ. The first nodes of at most 2 terms belong to any one owner, and those of exactly 2 terms to some owner.
All inputs are finite; a program needn't handle non-finite values.
Results may differ from the reference program's by a relative error of at most 0.000098.
Values sent between devices are 32-bit elements; how exact they have to be, the bound alone decides.
A program may use at most 64 MiB of HBM per device.

```python
import jax
import jax.numpy as jnp
from jax import lax

NODE_DEV = 2
ORDER = 512
SLOTS = 2
NODES = 8
TERMS = 4


def draw_term_nodes(key, part):
    owners = NODES // NODE_DEV
    key_bias, key_jitter, key_hot, key_order, key_local, key_other = jax.random.split(key, 6)
    levels = jax.random.randint(key_bias, (owners, 1), 0, 4) * 1024
    jitter = jax.random.randint(key_jitter, (owners, SLOTS), 0, 1024)
    hottest = jax.random.randint(key_hot, (), 0, owners)
    owner_grid = jnp.arange(owners, dtype=jnp.int32)[:, None] * jnp.ones((1, SLOTS), jnp.int32)
    scores = jnp.where(owner_grid == hottest, 4096, levels + jitter)
    unique = scores * (owners * SLOTS) + jnp.arange(owners * SLOTS, dtype=jnp.int32).reshape(owners, SLOTS)
    chosen = lax.top_k(unique.reshape(-1), TERMS)[1]
    shuffled = jax.random.permutation(key_order, chosen)
    leading = shuffled // SLOTS * NODE_DEV + jax.random.randint(key_local, (TERMS,), 0, NODE_DEV)
    second = (leading + 1 + jax.random.randint(key_other, (TERMS,), 0, NODES - 1)) % NODES
    return jnp.stack([leading, second], axis=1).astype(jnp.int32)


def set_ends(result, own_key, least, largest):
    longest = result.shape.index(max(result.shape))
    spots = []
    for shift in (0, 1):
        where = [jax.random.randint(jax.random.fold_in(own_key, axis), (), 0, length) for axis, length in enumerate(result.shape)]
        where[longest] = (where[longest] + shift) % result.shape[longest]
        spots.append(tuple(where))
    return result.at[spots[0]].set(least).at[spots[1]].set(largest)


def shard_levels(rng, dims, cuts, low, largest):
    gain, own = 1.0, jax.random.fold_in(rng, 6)
    for axis_at, shards_of in cuts:
        heights = jnp.exp(jax.random.uniform(jax.random.fold_in(own, axis_at), (shards_of,), jnp.float32, low / len(cuts), largest / len(cuts)))
        gain = gain * jnp.repeat(heights, dims[axis_at] // shards_of).reshape([-1 if axis == axis_at else 1 for axis in range(len(dims))])
    return gain


def centred(stream_key, shape, deviation, limit, cuts=(), kind=jnp.bfloat16):
    gain = shard_levels(stream_key, shape, cuts, -0.22, 0.18) if cuts else 1.0
    drawn = jax.random.normal(stream_key, shape, jnp.float32) * deviation * gain
    return jnp.minimum(jnp.maximum(drawn, -limit), limit).astype(kind)


def setup_inputs(seed: int = 0, part: int = 0) -> dict:
    key_of = jax.random.split(jax.random.key(seed), 5)
    part_splits = jax.random.split(jax.random.fold_in(key_of[4], part), 5)
    return {
        "meson_nodes": centred(part_splits[0], (2, NODES, ORDER, ORDER), 0.096, 0.66, ((1, 4), (2, 2), (3, 2)), jnp.float32),
        "term_nodes": draw_term_nodes(jax.random.fold_in(jax.random.fold_in(key_of[4], part), 71), part),
        "weight_codes": set_ends(jax.random.randint(part_splits[2], (TERMS,), 0, 8), jax.random.fold_in(part_splits[2], 1), 0, 7).astype(jnp.int32),
        "resident_pick": set_ends(jax.random.randint(part_splits[3], (NODES,), 0, NODE_DEV), jax.random.fold_in(part_splits[3], 1), 0, NODE_DEV - 1).astype(jnp.int32),
    }


def complex_product(left_matrix, right_matrix):
    highest = lax.Precision.HIGHEST
    real_part = jnp.dot(left_matrix[0], right_matrix[0], precision=highest, preferred_element_type=jnp.float32) - jnp.dot(left_matrix[1], right_matrix[1], precision=highest, preferred_element_type=jnp.float32)
    imag_part = jnp.dot(left_matrix[0], right_matrix[1], precision=highest, preferred_element_type=jnp.float32) + jnp.dot(left_matrix[1], right_matrix[0], precision=highest, preferred_element_type=jnp.float32)
    return jnp.stack([real_part, imag_part])


def reference(meson_nodes, term_nodes, weight_codes, resident_pick):
    factors = (weight_codes.astype(jnp.float32) - 3.5) * 0.5

    def one_term(pair_ids):
        return complex_product(meson_nodes[:, pair_ids[0]], meson_nodes[:, pair_ids[1]])

    products = lax.map(one_term, term_nodes)
    node_ids = jnp.arange(NODES, dtype=jnp.int32)
    incidence = (term_nodes[:, 0:1] == node_ids[None, :]).astype(jnp.float32) + (term_nodes[:, 1:2] == node_ids[None, :]).astype(jnp.float32)
    mixing = factors[:, None] * incidence
    summed = jnp.einsum("tn,tcij->cnij", mixing, products, precision=lax.Precision.HIGHEST)
    resident = (node_ids // NODE_DEV) * NODE_DEV + resident_pick

    def one_node(node_index):
        return complex_product(summed[:, node_index], meson_nodes[:, resident[node_index]])

    contracted = lax.map(one_node, node_ids)
    return jnp.transpose(contracted, (1, 0, 2, 3))
```

```python
import functools

import jax
import jax.numpy as jnp
from jax import lax
from jax.experimental import pallas as pl
from jax.experimental.pallas import tpu as pltpu
from jax.sharding import PartitionSpec as P


def complex_step(full_left, segment):
    highest = lax.Precision.HIGHEST
    real_part = jnp.einsum(
        "kij,kjl->kil",
        full_left[0],
        segment[0],
        precision=highest,
        preferred_element_type=jnp.float32,
    ) - jnp.einsum(
        "kij,kjl->kil",
        full_left[1],
        segment[1],
        precision=highest,
        preferred_element_type=jnp.float32,
    )
    imag_part = jnp.einsum(
        "kij,kjl->kil",
        full_left[0],
        segment[1],
        precision=highest,
        preferred_element_type=jnp.float32,
    ) + jnp.einsum(
        "kij,kjl->kil",
        full_left[1],
        segment[0],
        precision=highest,
        preferred_element_type=jnp.float32,
    )
    return jnp.stack([real_part, imag_part])


def wide_body(meson_nodes, term_nodes, weight_codes, resident_pick):
    node_count = lax.axis_size("node")
    owned = meson_nodes.shape[1]
    row_count = meson_nodes.shape[2]
    col_count = meson_nodes.shape[3]
    band = row_count // node_count
    total_nodes = owned * node_count
    term_count = term_nodes.shape[0]
    banded = meson_nodes.reshape(2, owned, node_count, band * col_count)
    spread = lax.all_to_all(banded, "node", split_axis=2, concat_axis=1, tiled=True).reshape(
        2, total_nodes, band * col_count
    )
    leading = term_nodes[:, 0]
    trailing = term_nodes[:, 1]
    worker_ids = jnp.arange(node_count, dtype=jnp.int32)
    slot_count = term_count // node_count
    table = jnp.arange(slot_count, dtype=jnp.int32)[None, :] * node_count + worker_ids[:, None]
    active = jnp.ones(table.shape, jnp.float32)
    first_table = leading[table]
    second_table = trailing[table]
    factors = active * (weight_codes[table].astype(jnp.float32) - 3.5) * 0.5
    wanted = jnp.stack([first_table.T, second_table.T], axis=1)
    picked = jnp.take(spread, wanted, axis=1)
    fetched = lax.all_to_all(picked, "node", split_axis=3, concat_axis=3, tiled=True).reshape(
        2, slot_count, 2, row_count, col_count
    )
    left_rows = fetched[:, :, 0]
    right_band = fetched[:, :, 1]
    left_full = lax.all_gather(left_rows, "rep", axis=3, tiled=True)
    products = complex_step(left_full, lax.all_gather(right_band, "sub", axis=2, tiled=True))
    outgoing = products.reshape(2, slot_count, node_count, band * col_count)
    returned = lax.all_to_all(outgoing, "node", split_axis=2, concat_axis=1, tiled=True).reshape(
        2, node_count * slot_count, band * col_count
    )
    node_ids = jnp.arange(total_nodes, dtype=jnp.int32)
    incidence = (first_table.reshape(-1)[:, None] == node_ids[None, :]).astype(jnp.float32) + (
        second_table.reshape(-1)[:, None] == node_ids[None, :]
    ).astype(jnp.float32)
    mixing = factors.reshape(-1)[:, None] * incidence
    summed = jnp.einsum("mn,cmx->cnx", mixing, returned, precision=lax.Precision.HIGHEST)
    owner_sum = lax.all_to_all(
        summed.reshape(2, total_nodes, 1, band * col_count),
        "node",
        split_axis=1,
        concat_axis=2,
        tiled=True,
    ).reshape(2, owned, row_count, col_count)
    sum_full = lax.all_gather(owner_sum, "rep", axis=3, tiled=True)
    own_index = lax.axis_index("node")
    picks = lax.dynamic_slice_in_dim(resident_pick, own_index * owned, owned)
    resident = jnp.take(meson_nodes, picks, axis=1)
    return complex_step(sum_full, lax.all_gather(resident, "sub", axis=2, tiled=True))


MESH = pl.DeviceIdType.MESH
FOREIGN = 2


def split(value):
    high = value.astype(jnp.bfloat16)
    return high, (value - high.astype(jnp.float32)).astype(jnp.bfloat16)


def mul(left, right):
    def dot(p, q):
        return jnp.dot(p, q, preferred_element_type=jnp.float32)

    return dot(left[0], right[0]) + (dot(left[0], right[1]) + dot(left[1], right[0]))


def complex_mul(lefts, rights):
    real = imag = None
    for (a0, a1), (b0, b1) in zip(lefts, rights):
        a0, a1, b0, b1 = split(a0), split(a1), split(b0), split(b1)
        re = mul(a0, b0) - mul(a1, b1)
        im = mul(a0, b1) + mul(a1, b0)
        real = re if real is None else real + re
        imag = im if imag is None else imag + im
    return real, imag


def line_kernel(
    length, owned, terms,
    x_ref, tn_ref, wc_ref, rp_ref, out_ref,
    nodes, rows, sums,
    loc_sem, z_send, z_recv, c_send, c_recv, x_send, x_recv, s_send, s_recv,
):
    z = lax.axis_index("node")
    x = lax.axis_index("sub")
    c = lax.axis_index("rep")
    g = lax.axis_index("grp")
    left = (g, z - 1, x, c)
    right = (g, z + 1, x, c)
    across = (g, z, 1 - x, c)
    twin = (g, z, x, 1 - c)
    has_left = z > 0
    has_right = z < length - 1
    pieces = [(j, m) for j in range(owned) for m in range(2)]

    def remote(src, dst, send, recv, device):
        return pltpu.make_async_remote_copy(
            src_ref=src, dst_ref=dst, send_sem=send, recv_sem=recv, device_id=device, device_id_type=MESH
        )

    barrier = pltpu.get_barrier_semaphore()
    for device in (across, twin):
        pl.semaphore_signal(barrier, inc=1, device_id=device, device_id_type=MESH)

    @pl.when(has_left)
    def _():
        pl.semaphore_signal(barrier, inc=1, device_id=left, device_id_type=MESH)

    @pl.when(has_right)
    def _():
        pl.semaphore_signal(barrier, inc=1, device_id=right, device_id_type=MESH)

    pl.semaphore_wait(barrier, 2 + has_left.astype(jnp.int32) + has_right.astype(jnp.int32))

    def node_at(owner, j, m):
        return nodes.at[c, owner * owned + j, m]

    def z_copy(way, step, j, m):
        owner = z + step if way == 0 else z - step
        src = x_ref.at[m, j] if step == 0 else node_at(owner, j, m)
        return remote(
            src, node_at(owner, j, m), z_send.at[way, step, j, m], z_recv.at[way, step, j, m],
            left if way == 0 else right,
        )

    def z_sends(way, step):
        if way == 0:
            return jnp.logical_and(has_left, z + step <= length - 1)
        return jnp.logical_and(has_right, z - step >= 0)

    def z_arrival(way, step, j, m):
        owner = z + 1 + step if way == 0 else z - 1 - step
        return remote(
            node_at(owner, j, m), node_at(owner, j, m), z_send.at[way, step, j, m], z_recv.at[way, step, j, m],
            left if way == 0 else right,
        )

    def c_copy(owner, j, m, own=False):
        src = x_ref.at[m, j] if own else node_at(owner, j, m)
        return remote(src, node_at(owner, j, m), c_send.at[owner, j, m], c_recv.at[owner, j, m], twin)

    def x_own(j, m):
        return remote(x_ref.at[m, j], rows.at[x, j, m], x_send.at[j, m], x_recv.at[j, m], across)

    def x_slot(s, m):
        k = owned + s
        return remote(rows.at[x, k, m], rows.at[x, k, m], x_send.at[k, m], x_recv.at[k, m], across)

    for j, m in pieces:
        for way in range(2):

            @pl.when(z_sends(way, 0))
            def _():
                z_copy(way, 0, j, m).start()

        x_own(j, m).start()
    local = []
    for j, m in pieces:
        for i, dst in enumerate((node_at(z, j, m), rows.at[x, j, m])):
            copy = pltpu.make_async_copy(x_ref.at[m, j], dst, loc_sem.at[i, j, m])
            copy.start()
            local.append(copy)
        c_copy(z, j, m, own=True).start()
    for copy in local:
        copy.wait()

    far = jnp.where(z < length // 2, length - 1, 0)
    late = far * owned + owned - 1
    firsts = [tn_ref[t, 0] for t in range(terms)]
    seconds = [tn_ref[t, 1] for t in range(terms)]
    home = z * owned

    def mine(n):
        return jnp.logical_and(n >= home, n < home + owned)

    needs = [jnp.logical_and(mine(a), jnp.logical_not(mine(b))) for a, b in zip(firsts, seconds)]
    slot1 = home
    for need, b in zip(needs, seconds):
        slot1 = jnp.where(jnp.logical_and(need, slot1 != late), b, slot1)
    slot0 = home
    for need, b in zip(needs, seconds):
        slot0 = jnp.where(jnp.logical_and(need, b != slot1), b, slot0)

    def stage(s, m):
        wanted = slot1 if s else slot0
        chosen = nodes[c, home, m]
        for k in range(length):
            owner = lax.rem(far + 1 + k, length)
            for j in range(owned):
                if s == 0 and k == length - 1 and j == owned - 1:
                    continue
                n = owner * owned + j
                chosen = jnp.where(wanted == n, nodes[c, n, m], chosen)
        rows[x, owned + s, m] = chosen
        x_slot(s, m).start()

    for step in range(length - 1):
        for j, m in pieces:
            for way in range(2):
                owner = z + 1 + step if way == 0 else z - 1 - step
                arrives = owner <= length - 1 if way == 0 else owner >= 0

                @pl.when(arrives)
                def _():
                    z_arrival(way, step, j, m).wait_recv()
                    c_copy(owner, j, m).start()

                if step < length - 2:

                    @pl.when(jnp.logical_and(arrives, z_sends(way, step + 1)))
                    def _():
                        z_copy(way, step + 1, j, m).start()

            if step == length - 2:
                stage(j, m)

    for owner in range(length):
        for j, m in pieces:
            remote(
                nodes.at[1 - c, owner * owned + j, m], nodes.at[1 - c, owner * owned + j, m],
                c_send.at[owner, j, m], c_recv.at[owner, j, m], twin,
            ).wait_recv()
    for k in range(owned + FOREIGN):
        for m in range(2):
            remote(
                rows.at[1 - x, k, m], rows.at[1 - x, k, m], x_send.at[k, m], x_recv.at[k, m], across
            ).wait_recv()

    for t in range(terms):
        a, b = firsts[t], seconds[t]
        k = jnp.where(mine(b), b - home, jnp.where(b == slot1, owned + 1, owned))
        real, imag = complex_mul(
            [(nodes[h, a, 0], nodes[h, a, 1]) for h in range(2)],
            [(rows[h, k, 0], rows[h, k, 1]) for h in range(2)],
        )
        factor = (wc_ref[t].astype(jnp.float32) - 3.5) * 0.5
        for j in range(owned):
            n = home + j
            count = (a == n).astype(jnp.float32) + (b == n).astype(jnp.float32)
            weight = factor * count
            for m, part in ((0, real), (1, imag)):
                if t == 0:
                    sums[c, j, m] = weight * part
                else:
                    sums[c, j, m] = sums[c, j, m] + weight * part

    def s_copy(h, j, m):
        return remote(sums.at[h, j, m], sums.at[h, j, m], s_send.at[j, m], s_recv.at[j, m], twin)

    for j, m in pieces:
        s_copy(c, j, m).start()
    for j, m in pieces:
        s_copy(1 - c, j, m).wait_recv()
    for j in range(owned):
        pick = rp_ref[home + j]
        real, imag = complex_mul(
            [(sums[h, j, 0], sums[h, j, 1]) for h in range(2)],
            [(rows[h, pick, 0], rows[h, pick, 1]) for h in range(2)],
        )
        out_ref[0, j] = real
        out_ref[1, j] = imag

    for j, m in pieces:
        s_copy(c, j, m).wait_send()
        x_own(j, m).wait_send()
    for s in range(FOREIGN):
        for m in range(2):
            x_slot(s, m).wait_send()
    for step in range(length - 1):
        for j, m in pieces:
            for way in range(2):

                @pl.when(z_sends(way, step))
                def _():
                    z_copy(way, step, j, m).wait_send()

    for owner in range(length):
        for j, m in pieces:
            c_copy(owner, j, m).wait_send()


def line_body(meson_nodes, term_nodes, weight_codes, resident_pick):
    length = lax.axis_size("node")
    _, owned, height, width = meson_nodes.shape
    terms = term_nodes.shape[0]
    block = (height, width)
    vmem = pl.BlockSpec(memory_space=pltpu.VMEM)
    smem = pl.BlockSpec(memory_space=pltpu.SMEM)
    dma = pltpu.SemaphoreType.DMA
    slots = owned + FOREIGN
    return pl.pallas_call(
        functools.partial(line_kernel, length, owned, terms),
        out_shape=jax.ShapeDtypeStruct(meson_nodes.shape, jnp.float32),
        in_specs=[pl.BlockSpec(memory_space=pl.ANY), smem, smem, smem],
        out_specs=vmem,
        scratch_shapes=[
            pltpu.VMEM((2, length * owned, 2) + block, jnp.float32),
            pltpu.VMEM((2, slots, 2) + block, jnp.float32),
            pltpu.VMEM((2, owned, 2) + block, jnp.float32),
            dma((2, owned, 2)),
            dma((2, length - 1, owned, 2)),
            dma((2, length - 1, owned, 2)),
            dma((length, owned, 2)),
            dma((length, owned, 2)),
            dma((slots, 2)),
            dma((slots, 2)),
            dma((owned, 2)),
            dma((owned, 2)),
        ],
        compiler_params=pltpu.CompilerParams(
            collective_id=0, has_side_effects=True, vmem_limit_bytes=56 << 20
        ),
    )(meson_nodes, term_nodes, weight_codes, resident_pick)


def body(meson_nodes, term_nodes, weight_codes, resident_pick):
    length, owned = lax.axis_size("node"), meson_nodes.shape[1]
    square = meson_nodes.shape[2] == meson_nodes.shape[3]
    halves = lax.axis_size("sub") == 2 and lax.axis_size("rep") == 2
    held = 2 * length * meson_nodes.size * 4
    fits = held <= 16 << 20 and term_nodes.shape[0] <= 8
    if square and halves and fits and owned == FOREIGN and length > 2:
        return line_body(meson_nodes, term_nodes, weight_codes, resident_pick)
    return wide_body(meson_nodes, term_nodes, weight_codes, resident_pick)


def solution(mesh):
    in_specs = (P(None, ("grp", "node"), "sub", "rep"), P("grp", None), P("grp"), P("grp"))
    out_specs = P(None, ("grp", "node"), "sub", "rep")
    return jax.shard_map(body, mesh=mesh, in_specs=in_specs, out_specs=out_specs, check_vma=False)
```

```python
import functools

import jax
import jax.numpy as jnp
from jax import lax
from jax.experimental import pallas as pl
from jax.experimental.pallas import tpu as pltpu
from jax.sharding import PartitionSpec as P


def complex_step(full_left, segment):
    highest = lax.Precision.HIGHEST
    real_part = jnp.einsum(
        "kij,kjl->kil",
        full_left[0],
        segment[0],
        precision=highest,
        preferred_element_type=jnp.float32,
    ) - jnp.einsum(
        "kij,kjl->kil",
        full_left[1],
        segment[1],
        precision=highest,
        preferred_element_type=jnp.float32,
    )
    imag_part = jnp.einsum(
        "kij,kjl->kil",
        full_left[0],
        segment[1],
        precision=highest,
        preferred_element_type=jnp.float32,
    ) + jnp.einsum(
        "kij,kjl->kil",
        full_left[1],
        segment[0],
        precision=highest,
        preferred_element_type=jnp.float32,
    )
    return jnp.stack([real_part, imag_part])


def wide_body(meson_nodes, term_nodes, weight_codes, resident_pick):
    node_count = lax.axis_size("node")
    owned = meson_nodes.shape[1]
    row_count = meson_nodes.shape[2]
    col_count = meson_nodes.shape[3]
    band = row_count // node_count
    total_nodes = owned * node_count
    term_count = term_nodes.shape[0]
    banded = meson_nodes.reshape(2, owned, node_count, band * col_count)
    spread = lax.all_to_all(banded, "node", split_axis=2, concat_axis=1, tiled=True).reshape(
        2, total_nodes, band * col_count
    )
    leading = term_nodes[:, 0]
    trailing = term_nodes[:, 1]
    worker_ids = jnp.arange(node_count, dtype=jnp.int32)
    slot_count = term_count // node_count
    table = jnp.arange(slot_count, dtype=jnp.int32)[None, :] * node_count + worker_ids[:, None]
    active = jnp.ones(table.shape, jnp.float32)
    first_table = leading[table]
    second_table = trailing[table]
    factors = active * (weight_codes[table].astype(jnp.float32) - 3.5) * 0.5
    wanted = jnp.stack([first_table.T, second_table.T], axis=1)
    picked = jnp.take(spread, wanted, axis=1)
    fetched = lax.all_to_all(picked, "node", split_axis=3, concat_axis=3, tiled=True).reshape(
        2, slot_count, 2, row_count, col_count
    )
    left_rows = fetched[:, :, 0]
    right_band = fetched[:, :, 1]
    left_full = lax.all_gather(left_rows, "rep", axis=3, tiled=True)
    products = complex_step(left_full, lax.all_gather(right_band, "sub", axis=2, tiled=True))
    outgoing = products.reshape(2, slot_count, node_count, band * col_count)
    returned = lax.all_to_all(outgoing, "node", split_axis=2, concat_axis=1, tiled=True).reshape(
        2, node_count * slot_count, band * col_count
    )
    node_ids = jnp.arange(total_nodes, dtype=jnp.int32)
    incidence = (first_table.reshape(-1)[:, None] == node_ids[None, :]).astype(jnp.float32) + (
        second_table.reshape(-1)[:, None] == node_ids[None, :]
    ).astype(jnp.float32)
    mixing = factors.reshape(-1)[:, None] * incidence
    summed = jnp.einsum("mn,cmx->cnx", mixing, returned, precision=lax.Precision.HIGHEST)
    owner_sum = lax.all_to_all(
        summed.reshape(2, total_nodes, 1, band * col_count),
        "node",
        split_axis=1,
        concat_axis=2,
        tiled=True,
    ).reshape(2, owned, row_count, col_count)
    sum_full = lax.all_gather(owner_sum, "rep", axis=3, tiled=True)
    own_index = lax.axis_index("node")
    picks = lax.dynamic_slice_in_dim(resident_pick, own_index * owned, owned)
    resident = jnp.take(meson_nodes, picks, axis=1)
    return complex_step(sum_full, lax.all_gather(resident, "sub", axis=2, tiled=True))


MESH = pl.DeviceIdType.MESH
PIECES = 2
FOREIGN = 2


def split(value):
    high = value.astype(jnp.bfloat16)
    return high, (value - high.astype(jnp.float32)).astype(jnp.bfloat16)


def mul(left, right):
    def dot(p, q):
        return jnp.dot(p, q, preferred_element_type=jnp.float32)

    return dot(left[0], right[0]) + (dot(left[0], right[1]) + dot(left[1], right[0]))


def complex_mul(a0, a1, b0, b1):
    left, right = split(a0), split(b0)
    both = mul(left, right)
    left, right = split(a1), split(b1)
    other = mul(left, right)
    cross = mul(split(a0 + a1), split(b0 + b1))
    return both - other, cross - both - other


def line_kernel(
    length, owned, terms,
    x_ref, tn_ref, wc_ref, rp_ref, out_ref,
    nodes, rows, others, sums, picked,
    loc_sem, z_send, z_recv, c_send, c_recv, x_send, x_recv, s_send, s_recv,
):
    z = lax.axis_index("node")
    x = lax.axis_index("sub")
    c = lax.axis_index("rep")
    g = lax.axis_index("grp")
    left = (g, z - 1, x, c)
    right = (g, z + 1, x, c)
    across = (g, z, 1 - x, c)
    twin = (g, z, x, 1 - c)
    has_left = z > 0
    has_right = z < length - 1
    height = x_ref.shape[2] // PIECES
    pieces = [(j, m, r) for j in range(owned) for m in range(2) for r in range(PIECES)]

    def band(r):
        return pl.ds(r * height, height)

    def remote(src, dst, send, recv, device):
        return pltpu.make_async_remote_copy(
            src_ref=src, dst_ref=dst, send_sem=send, recv_sem=recv, device_id=device, device_id_type=MESH
        )

    barrier = pltpu.get_barrier_semaphore()
    for device in (across, twin):
        pl.semaphore_signal(barrier, inc=1, device_id=device, device_id_type=MESH)

    @pl.when(has_left)
    def _():
        pl.semaphore_signal(barrier, inc=1, device_id=left, device_id_type=MESH)

    @pl.when(has_right)
    def _():
        pl.semaphore_signal(barrier, inc=1, device_id=right, device_id_type=MESH)

    pl.semaphore_wait(barrier, 2 + has_left.astype(jnp.int32) + has_right.astype(jnp.int32))

    def node_at(owner, j, m, r):
        return nodes.at[c, owner * owned + j, m, band(r)]

    def own_at(j, m, r):
        return x_ref.at[m, j, band(r)]

    def reach(way, step):
        return z + step if way == 0 else z - step

    def inside(owner):
        return jnp.logical_and(owner >= 0, owner <= length - 1)

    def to_end(way):
        return z == (1 if way == 0 else length - 2)

    def z_sends(way, step):
        found = jnp.logical_and(has_left if way == 0 else has_right, inside(reach(way, step)))
        return jnp.logical_and(found, jnp.logical_not(to_end(way))) if step == 0 else found

    def z_arrives(way, step):
        found = inside(reach(way, step + 1))
        return jnp.logical_and(found, z != (0 if way == 0 else length - 1)) if step == 0 else found

    def z_copy(way, step, j, m, r, src):
        return remote(
            src, node_at(reach(way, step), j, m, r), z_send.at[way, step, j, m, r],
            z_recv.at[way, step, j, m, r], left if way == 0 else right,
        )

    def c_copy(owner, j, m, r, src):
        return remote(
            src, node_at(owner, j, m, r), c_send.at[owner, j, m, r], c_recv.at[owner, j, m, r], twin
        )

    def x_copy(k, m, r, src):
        return remote(src, others.at[k, m, band(r)], x_send.at[k, m, r], x_recv.at[k, m, r], across)

    def s_copy(h, j, m):
        return remote(sums.at[h, j, m], sums.at[h, j, m], s_send.at[j, m], s_recv.at[j, m], twin)

    for way in range(2):

        @pl.when(z_sends(way, 0))
        def _():
            for piece in pieces:
                z_copy(way, 0, *piece, own_at(*piece)).start()

    for piece in pieces:
        x_copy(*piece, own_at(*piece)).start()
    local = []
    for j, m, r in pieces:
        for i, dst in enumerate((node_at(z, j, m, r), rows.at[j, m, band(r)])):
            copy = pltpu.make_async_copy(own_at(j, m, r), dst, loc_sem.at[i, j, m, r])
            copy.start()
            local.append(copy)
        c_copy(z, j, m, r, own_at(j, m, r)).start()

    firsts = [tn_ref[t, 0] for t in range(terms)]
    seconds = [tn_ref[t, 1] for t in range(terms)]
    spots = (length - 2) * owned

    def holds(owner, n):
        return jnp.logical_and(n >= owner * owned, n < owner * owned + owned)

    def rank_of(end, n):
        owner = n // owned
        return jnp.where(end == 0, owner, length - 1 - owner) * owned + n - owner * owned

    def node_of(end, rank):
        far = rank // owned
        return jnp.where(end == 0, far, length - 1 - far) * owned + rank % owned

    def partner_ranks(end):
        ranks = []
        for a, b in zip(firsts, seconds):
            here, there = holds(end, a), holds(end, b)
            rank = jnp.where(here, rank_of(end, b), rank_of(end, a))
            ranks.append(jnp.where(here != there, rank, owned))
        below, found = length * owned, []
        for _ in range(spots):
            best = owned
            for rank in ranks:
                best = jnp.where(jnp.logical_and(rank < below, rank > best), rank, best)
            found.append(best)
            below = best
        return found[::-1]

    end = jnp.where(z < length // 2, 0, length - 1)
    wanted_ranks = partner_ranks(end)
    at_end = z == end

    def entry(n):
        place = z * owned
        rank = rank_of(end, n)
        for i in range(spots):
            place = jnp.where(wanted_ranks[i] == rank, node_of(end, 2 * owned + i), place)
        return jnp.where(jnp.logical_and(at_end, jnp.logical_not(holds(z, n))), place, n)

    far = length - 1 - end
    late = far * owned + owned - 1
    home = z * owned
    left_entries = [entry(a) for a in firsts]
    right_entries = [entry(b) for b in seconds]
    needs = [
        jnp.logical_and(holds(z, a), jnp.logical_not(holds(z, b))) for a, b in zip(firsts, seconds)
    ]
    slot1 = home
    for need, e in zip(needs, right_entries):
        slot1 = jnp.where(jnp.logical_and(need, slot1 != late), e, slot1)
    slot0 = home
    for need, e in zip(needs, right_entries):
        slot0 = jnp.where(jnp.logical_and(need, e != slot1), e, slot0)

    for copy in local:
        copy.wait()

    def pick(i, m, r):
        chosen = nodes[c, node_of(end, owned), m, band(r)]
        for rank in range(owned + 1, 2 * owned + i + 1):
            chosen = jnp.where(
                wanted_ranks[i] == rank, nodes[c, node_of(end, rank), m, band(r)], chosen
            )
        picked[i, m, band(r)] = chosen

    def stage(s, m, r):
        wanted = slot1 if s else slot0
        chosen = nodes[c, home, m, band(r)]
        for k in range(length):
            owner = lax.rem(far + 1 + k, length)
            for j in range(owned):
                if s == 0 and k == length - 1 and j == owned - 1:
                    continue
                n = owner * owned + j
                chosen = jnp.where(wanted == n, nodes[c, n, m, band(r)], chosen)
        rows[owned + s, m, band(r)] = chosen
        x_copy(owned + s, m, r, rows.at[owned + s, m, band(r)]).start()

    depth = jnp.maximum(z, length - 1 - z) - 1
    for step in range(length - 1):
        for j, m, r in pieces:
            for way in range(2):

                @pl.when(z_arrives(way, step))
                def _():
                    owner = reach(way, step + 1)
                    src = node_at(owner, j, m, r)
                    remote(
                        src, src, z_send.at[way, step, j, m, r], z_recv.at[way, step, j, m, r],
                        left if way == 0 else right,
                    ).wait_recv()
                    c_copy(owner, j, m, r, src).start()

                if step < length - 2:
                    goes = jnp.logical_and(z_arrives(way, step), z_sends(way, step + 1))

                    @pl.when(jnp.logical_and(goes, jnp.logical_not(to_end(way))))
                    def _():
                        z_copy(way, step + 1, j, m, r, node_at(reach(way, step + 1), j, m, r)).start()

                    @pl.when(jnp.logical_and(goes, to_end(way)))
                    def _():
                        i = step * owned + j
                        pick(i, m, r)
                        z_copy(way, step + 1, j, m, r, picked.at[i, m, band(r)]).start()

            if step >= length // 2 - 1:

                @pl.when(depth == step)
                def _():
                    stage(j, m, r)

    def filled(owner):
        beside = jnp.where(end == 0, 1, length - 2)
        return jnp.logical_not(jnp.logical_and(at_end, owner == beside))

    for owner in range(length):

        @pl.when(filled(owner))
        def _():
            for j, m, r in pieces:
                dst = nodes.at[1 - c, owner * owned + j, m, band(r)]
                remote(dst, dst, c_send.at[owner, j, m, r], c_recv.at[owner, j, m, r], twin).wait_recv()

    def products(h, held, fresh):
        for t in range(terms):
            a, b = firsts[t], seconds[t]
            e, f = left_entries[t], right_entries[t]
            k = jnp.where(holds(z, b), b - home, jnp.where(f == slot1, owned + 1, owned))
            parts = complex_mul(nodes[h, e, 0], nodes[h, e, 1], held[k, 0], held[k, 1])
            factor = (wc_ref[t].astype(jnp.float32) - 3.5) * 0.5
            for j in range(owned):
                n = home + j
                count = (a == n).astype(jnp.float32) + (b == n).astype(jnp.float32)
                weight = factor * count
                for m in range(2):
                    if t == 0 and fresh:
                        sums[c, j, m] = weight * parts[m]
                    else:
                        sums[c, j, m] = sums[c, j, m] + weight * parts[m]

    products(x, rows, True)
    for k in range(owned + FOREIGN):
        for m in range(2):
            for r in range(PIECES):
                dst = others.at[k, m, band(r)]
                remote(dst, dst, x_send.at[k, m, r], x_recv.at[k, m, r], across).wait_recv()
    products(1 - x, others, False)

    for j in range(owned):
        for m in range(2):
            s_copy(c, j, m).start()
    for h in (c, 1 - c):
        for j in range(owned):
            if h is not c:
                for m in range(2):
                    s_copy(h, j, m).wait_recv()
            choice = rp_ref[home + j]
            here = [jnp.where(h == x, rows[choice, m], others[choice, m]) for m in range(2)]
            parts = complex_mul(sums[h, j, 0], sums[h, j, 1], here[0], here[1])
            for m in range(2):
                out_ref[m, j] = parts[m] if h is c else out_ref[m, j] + parts[m]

    for j in range(owned):
        for m in range(2):
            s_copy(c, j, m).wait_send()
    for piece in pieces:
        x_copy(*piece, own_at(*piece)).wait_send()
    for s in range(FOREIGN):
        for m in range(2):
            for r in range(PIECES):
                x_copy(owned + s, m, r, rows.at[owned + s, m, band(r)]).wait_send()
    for step in range(length - 1):
        for way in range(2):

            @pl.when(z_sends(way, step))
            def _():
                for piece in pieces:
                    z_copy(way, step, *piece, own_at(*piece)).wait_send()

    for owner in range(length):

        @pl.when(filled(owner))
        def _():
            for piece in pieces:
                c_copy(owner, *piece, own_at(*piece)).wait_send()


def line_body(meson_nodes, term_nodes, weight_codes, resident_pick):
    length = lax.axis_size("node")
    _, owned, height, width = meson_nodes.shape
    terms = term_nodes.shape[0]
    block = (height, width)
    vmem = pl.BlockSpec(memory_space=pltpu.VMEM)
    smem = pl.BlockSpec(memory_space=pltpu.SMEM)
    dma = pltpu.SemaphoreType.DMA
    slots = owned + FOREIGN
    return pl.pallas_call(
        functools.partial(line_kernel, length, owned, terms),
        out_shape=jax.ShapeDtypeStruct(meson_nodes.shape, jnp.float32),
        in_specs=[pl.BlockSpec(memory_space=pl.ANY), smem, smem, smem],
        out_specs=vmem,
        scratch_shapes=[
            pltpu.VMEM((2, length * owned, 2) + block, jnp.float32),
            pltpu.VMEM((slots, 2) + block, jnp.float32),
            pltpu.VMEM((slots, 2) + block, jnp.float32),
            pltpu.VMEM((2, owned, 2) + block, jnp.float32),
            pltpu.VMEM(((length - 2) * owned, 2) + block, jnp.float32),
            dma((2, owned, 2, PIECES)),
            dma((2, length - 1, owned, 2, PIECES)),
            dma((2, length - 1, owned, 2, PIECES)),
            dma((length, owned, 2, PIECES)),
            dma((length, owned, 2, PIECES)),
            dma((slots, 2, PIECES)),
            dma((slots, 2, PIECES)),
            dma((owned, 2)),
            dma((owned, 2)),
        ],
        compiler_params=pltpu.CompilerParams(
            collective_id=0, has_side_effects=True, vmem_limit_bytes=56 << 20
        ),
    )(meson_nodes, term_nodes, weight_codes, resident_pick)


def body(meson_nodes, term_nodes, weight_codes, resident_pick):
    length, owned = lax.axis_size("node"), meson_nodes.shape[1]
    square = meson_nodes.shape[2] == meson_nodes.shape[3]
    halves = lax.axis_size("sub") == 2 and lax.axis_size("rep") == 2
    held = 2 * length * meson_nodes.size * 4
    fits = held <= 16 << 20 and term_nodes.shape[0] <= (length - 2) * owned
    if square and halves and fits and owned == FOREIGN and length == 4:
        return line_body(meson_nodes, term_nodes, weight_codes, resident_pick)
    return wide_body(meson_nodes, term_nodes, weight_codes, resident_pick)


def solution(mesh):
    in_specs = (P(None, ("grp", "node"), "sub", "rep"), P("grp", None), P("grp"), P("grp"))
    out_specs = P(None, ("grp", "node"), "sub", "rep")
    return jax.shard_map(body, mesh=mesh, in_specs=in_specs, out_specs=out_specs, check_vma=False)
```

```python
import functools

import jax
import jax.numpy as jnp
from jax import lax
from jax.experimental import pallas as pl
from jax.experimental.pallas import tpu as pltpu
from jax.sharding import PartitionSpec as P


def complex_step(full_left, segment):
    highest = lax.Precision.HIGHEST
    real_part = jnp.einsum(
        "kij,kjl->kil",
        full_left[0],
        segment[0],
        precision=highest,
        preferred_element_type=jnp.float32,
    ) - jnp.einsum(
        "kij,kjl->kil",
        full_left[1],
        segment[1],
        precision=highest,
        preferred_element_type=jnp.float32,
    )
    imag_part = jnp.einsum(
        "kij,kjl->kil",
        full_left[0],
        segment[1],
        precision=highest,
        preferred_element_type=jnp.float32,
    ) + jnp.einsum(
        "kij,kjl->kil",
        full_left[1],
        segment[0],
        precision=highest,
        preferred_element_type=jnp.float32,
    )
    return jnp.stack([real_part, imag_part])


def wide_body(meson_nodes, term_nodes, weight_codes, resident_pick):
    node_count = lax.axis_size("node")
    owned = meson_nodes.shape[1]
    row_count = meson_nodes.shape[2]
    col_count = meson_nodes.shape[3]
    band = row_count // node_count
    total_nodes = owned * node_count
    term_count = term_nodes.shape[0]
    banded = meson_nodes.reshape(2, owned, node_count, band * col_count)
    spread = lax.all_to_all(banded, "node", split_axis=2, concat_axis=1, tiled=True).reshape(
        2, total_nodes, band * col_count
    )
    leading = term_nodes[:, 0]
    trailing = term_nodes[:, 1]
    worker_ids = jnp.arange(node_count, dtype=jnp.int32)
    slot_count = term_count // node_count
    table = jnp.arange(slot_count, dtype=jnp.int32)[None, :] * node_count + worker_ids[:, None]
    active = jnp.ones(table.shape, jnp.float32)
    first_table = leading[table]
    second_table = trailing[table]
    factors = active * (weight_codes[table].astype(jnp.float32) - 3.5) * 0.5
    wanted = jnp.stack([first_table.T, second_table.T], axis=1)
    picked = jnp.take(spread, wanted, axis=1)
    fetched = lax.all_to_all(picked, "node", split_axis=3, concat_axis=3, tiled=True).reshape(
        2, slot_count, 2, row_count, col_count
    )
    left_rows = fetched[:, :, 0]
    right_band = fetched[:, :, 1]
    left_full = lax.all_gather(left_rows, "rep", axis=3, tiled=True)
    products = complex_step(left_full, lax.all_gather(right_band, "sub", axis=2, tiled=True))
    outgoing = products.reshape(2, slot_count, node_count, band * col_count)
    returned = lax.all_to_all(outgoing, "node", split_axis=2, concat_axis=1, tiled=True).reshape(
        2, node_count * slot_count, band * col_count
    )
    node_ids = jnp.arange(total_nodes, dtype=jnp.int32)
    incidence = (first_table.reshape(-1)[:, None] == node_ids[None, :]).astype(jnp.float32) + (
        second_table.reshape(-1)[:, None] == node_ids[None, :]
    ).astype(jnp.float32)
    mixing = factors.reshape(-1)[:, None] * incidence
    summed = jnp.einsum("mn,cmx->cnx", mixing, returned, precision=lax.Precision.HIGHEST)
    owner_sum = lax.all_to_all(
        summed.reshape(2, total_nodes, 1, band * col_count),
        "node",
        split_axis=1,
        concat_axis=2,
        tiled=True,
    ).reshape(2, owned, row_count, col_count)
    sum_full = lax.all_gather(owner_sum, "rep", axis=3, tiled=True)
    own_index = lax.axis_index("node")
    picks = lax.dynamic_slice_in_dim(resident_pick, own_index * owned, owned)
    resident = jnp.take(meson_nodes, picks, axis=1)
    return complex_step(sum_full, lax.all_gather(resident, "sub", axis=2, tiled=True))


MESH = pl.DeviceIdType.MESH
PIECES = 4
FOREIGN = 2


def split(value):
    high = value.astype(jnp.bfloat16)
    return high, (value - high.astype(jnp.float32)).astype(jnp.bfloat16)


def mul(left, right):
    def dot(p, q):
        return jnp.dot(p, q, preferred_element_type=jnp.float32)

    return dot(left[0], right[0]) + (dot(left[0], right[1]) + dot(left[1], right[0]))


def complex_mul(a0, a1, b0, b1):
    left, right = split(a0), split(b0)
    both = mul(left, right)
    left, right = split(a1), split(b1)
    other = mul(left, right)
    cross = mul(split(a0 + a1), split(b0 + b1))
    return both - other, cross - both - other


def line_kernel(
    length, owned, terms,
    x_ref, tn_ref, wc_ref, rp_ref, out_ref,
    nodes, rows, others, sums, picked,
    loc_sem, z_send, z_recv, c_send, c_recv, x_send, x_recv, s_send, s_recv,
):
    z = lax.axis_index("node")
    x = lax.axis_index("sub")
    c = lax.axis_index("rep")
    g = lax.axis_index("grp")
    left = (g, z - 1, x, c)
    right = (g, z + 1, x, c)
    across = (g, z, 1 - x, c)
    twin = (g, z, x, 1 - c)
    has_left = z > 0
    has_right = z < length - 1
    height = x_ref.shape[2] // PIECES
    pieces = [(j, m, r) for j in range(owned) for m in range(2) for r in range(PIECES)]

    def band(r):
        return pl.ds(r * height, height)

    def remote(src, dst, send, recv, device):
        return pltpu.make_async_remote_copy(
            src_ref=src, dst_ref=dst, send_sem=send, recv_sem=recv, device_id=device, device_id_type=MESH
        )

    barrier = pltpu.get_barrier_semaphore()
    for device in (across, twin):
        pl.semaphore_signal(barrier, inc=1, device_id=device, device_id_type=MESH)

    @pl.when(has_left)
    def _():
        pl.semaphore_signal(barrier, inc=1, device_id=left, device_id_type=MESH)

    @pl.when(has_right)
    def _():
        pl.semaphore_signal(barrier, inc=1, device_id=right, device_id_type=MESH)

    pl.semaphore_wait(barrier, 2 + has_left.astype(jnp.int32) + has_right.astype(jnp.int32))

    def node_at(owner, j, m, r):
        return nodes.at[c, owner * owned + j, m, band(r)]

    def own_at(j, m, r):
        return x_ref.at[m, j, band(r)]

    def reach(way, step):
        return z + step if way == 0 else z - step

    def inside(owner):
        return jnp.logical_and(owner >= 0, owner <= length - 1)

    def to_end(way):
        return z == (1 if way == 0 else length - 2)

    def z_sends(way, step):
        found = jnp.logical_and(has_left if way == 0 else has_right, inside(reach(way, step)))
        return jnp.logical_and(found, jnp.logical_not(to_end(way))) if step == 0 else found

    def z_arrives(way, step):
        found = inside(reach(way, step + 1))
        return jnp.logical_and(found, z != (0 if way == 0 else length - 1)) if step == 0 else found

    def z_copy(way, step, j, m, r, src):
        return remote(
            src, node_at(reach(way, step), j, m, r), z_send.at[way, step, j, m, r],
            z_recv.at[way, step, j, m, r], left if way == 0 else right,
        )

    def c_copy(owner, j, m, r, src):
        return remote(
            src, node_at(owner, j, m, r), c_send.at[owner, j, m, r], c_recv.at[owner, j, m, r], twin
        )

    def x_copy(k, m, r, src):
        return remote(src, others.at[k, m, band(r)], x_send.at[k, m, r], x_recv.at[k, m, r], across)

    def s_copy(h, j, m):
        return remote(sums.at[h, j, m], sums.at[h, j, m], s_send.at[j, m], s_recv.at[j, m], twin)

    for way in range(2):

        @pl.when(z_sends(way, 0))
        def _():
            for piece in pieces:
                z_copy(way, 0, *piece, own_at(*piece)).start()

    for piece in pieces:
        x_copy(*piece, own_at(*piece)).start()
    local = []
    for j, m, r in pieces:
        for i, dst in enumerate((node_at(z, j, m, r), rows.at[j, m, band(r)])):
            copy = pltpu.make_async_copy(own_at(j, m, r), dst, loc_sem.at[i, j, m, r])
            copy.start()
            local.append(copy)
        c_copy(z, j, m, r, own_at(j, m, r)).start()

    firsts = [tn_ref[0, t] for t in range(terms)]
    seconds = [tn_ref[1, t] for t in range(terms)]
    spots = (length - 2) * owned

    def holds(owner, n):
        return jnp.logical_and(n >= owner * owned, n < owner * owned + owned)

    def rank_of(end, n):
        owner = n // owned
        return jnp.where(end == 0, owner, length - 1 - owner) * owned + n - owner * owned

    def node_of(end, rank):
        far = rank // owned
        return jnp.where(end == 0, far, length - 1 - far) * owned + rank % owned

    def partner_ranks(end):
        ranks = []
        for a, b in zip(firsts, seconds):
            here, there = holds(end, a), holds(end, b)
            rank = jnp.where(here, rank_of(end, b), rank_of(end, a))
            ranks.append(jnp.where(here != there, rank, owned))
        below, found = length * owned, []
        for _ in range(spots):
            best = owned
            for rank in ranks:
                best = jnp.where(jnp.logical_and(rank < below, rank > best), rank, best)
            found.append(best)
            below = best
        return found[::-1]

    end = jnp.where(z < length // 2, 0, length - 1)
    wanted_ranks = partner_ranks(end)
    at_end = z == end

    def entry(n):
        place = z * owned
        rank = rank_of(end, n)
        for i in range(spots):
            place = jnp.where(wanted_ranks[i] == rank, node_of(end, 2 * owned + i), place)
        return jnp.where(jnp.logical_and(at_end, jnp.logical_not(holds(z, n))), place, n)

    far = length - 1 - end
    late = far * owned + owned - 1
    home = z * owned
    left_entries = [entry(a) for a in firsts]
    right_entries = [entry(b) for b in seconds]
    needs = [
        jnp.logical_and(holds(z, a), jnp.logical_not(holds(z, b))) for a, b in zip(firsts, seconds)
    ]
    slot1 = home
    for need, e in zip(needs, right_entries):
        slot1 = jnp.where(jnp.logical_and(need, slot1 != late), e, slot1)
    slot0 = home
    for need, e in zip(needs, right_entries):
        slot0 = jnp.where(jnp.logical_and(need, e != slot1), e, slot0)

    for copy in local:
        copy.wait()

    def pick(i, m, r):
        chosen = nodes[c, node_of(end, owned), m, band(r)]
        for rank in range(owned + 1, 2 * owned + i + 1):
            chosen = jnp.where(
                wanted_ranks[i] == rank, nodes[c, node_of(end, rank), m, band(r)], chosen
            )
        picked[i, m, band(r)] = chosen

    def stage(s, m, r):
        wanted = slot1 if s else slot0
        chosen = nodes[c, home, m, band(r)]
        for k in range(length):
            owner = lax.rem(far + 1 + k, length)
            for j in range(owned):
                if s == 0 and k == length - 1 and j == owned - 1:
                    continue
                n = owner * owned + j
                chosen = jnp.where(wanted == n, nodes[c, n, m, band(r)], chosen)
        rows[owned + s, m, band(r)] = chosen
        x_copy(owned + s, m, r, rows.at[owned + s, m, band(r)]).start()

    depth = jnp.maximum(z, length - 1 - z) - 1
    for step in range(length - 1):
        for j, m, r in pieces:
            for way in range(2):

                @pl.when(z_arrives(way, step))
                def _():
                    owner = reach(way, step + 1)
                    src = node_at(owner, j, m, r)
                    remote(
                        src, src, z_send.at[way, step, j, m, r], z_recv.at[way, step, j, m, r],
                        left if way == 0 else right,
                    ).wait_recv()
                    c_copy(owner, j, m, r, src).start()

                if step < length - 2:
                    goes = jnp.logical_and(z_arrives(way, step), z_sends(way, step + 1))

                    @pl.when(jnp.logical_and(goes, jnp.logical_not(to_end(way))))
                    def _():
                        z_copy(way, step + 1, j, m, r, node_at(reach(way, step + 1), j, m, r)).start()

                    @pl.when(jnp.logical_and(goes, to_end(way)))
                    def _():
                        i = step * owned + j
                        pick(i, m, r)
                        z_copy(way, step + 1, j, m, r, picked.at[i, m, band(r)]).start()

            if step >= length // 2 - 1:

                @pl.when(depth == step)
                def _():
                    stage(j, m, r)

    def filled(owner):
        beside = jnp.where(end == 0, 1, length - 2)
        return jnp.logical_not(jnp.logical_and(at_end, owner == beside))

    for owner in range(length):

        @pl.when(filled(owner))
        def _():
            for j, m, r in pieces:
                dst = nodes.at[1 - c, owner * owned + j, m, band(r)]
                remote(dst, dst, c_send.at[owner, j, m, r], c_recv.at[owner, j, m, r], twin).wait_recv()

    def products(h, held, fresh):
        for t in range(terms):
            a, b = firsts[t], seconds[t]
            e, f = left_entries[t], right_entries[t]
            k = jnp.where(holds(z, b), b - home, jnp.where(f == slot1, owned + 1, owned))
            parts = complex_mul(nodes[h, e, 0], nodes[h, e, 1], held[k, 0], held[k, 1])
            factor = (wc_ref[t].astype(jnp.float32) - 3.5) * 0.5
            for j in range(owned):
                n = home + j
                count = (a == n).astype(jnp.float32) + (b == n).astype(jnp.float32)
                weight = factor * count
                for m in range(2):
                    if t == 0 and fresh:
                        sums[c, j, m] = weight * parts[m]
                    else:
                        sums[c, j, m] = sums[c, j, m] + weight * parts[m]

    products(x, rows, True)
    for k in range(owned + FOREIGN):
        for m in range(2):
            for r in range(PIECES):
                dst = others.at[k, m, band(r)]
                remote(dst, dst, x_send.at[k, m, r], x_recv.at[k, m, r], across).wait_recv()
    products(1 - x, others, False)

    for j in range(owned):
        for m in range(2):
            s_copy(c, j, m).start()
    for h in (c, 1 - c):
        for j in range(owned):
            if h is not c:
                for m in range(2):
                    s_copy(h, j, m).wait_recv()
            choice = rp_ref[home + j]
            here = [jnp.where(h == x, rows[choice, m], others[choice, m]) for m in range(2)]
            parts = complex_mul(sums[h, j, 0], sums[h, j, 1], here[0], here[1])
            for m in range(2):
                out_ref[m, j] = parts[m] if h is c else out_ref[m, j] + parts[m]

    for j in range(owned):
        for m in range(2):
            s_copy(c, j, m).wait_send()
    for piece in pieces:
        x_copy(*piece, own_at(*piece)).wait_send()
    for s in range(FOREIGN):
        for m in range(2):
            for r in range(PIECES):
                x_copy(owned + s, m, r, rows.at[owned + s, m, band(r)]).wait_send()
    for step in range(length - 1):
        for way in range(2):

            @pl.when(z_sends(way, step))
            def _():
                for piece in pieces:
                    z_copy(way, step, *piece, own_at(*piece)).wait_send()

    for owner in range(length):

        @pl.when(filled(owner))
        def _():
            for piece in pieces:
                c_copy(owner, *piece, own_at(*piece)).wait_send()


def line_body(meson_nodes, term_nodes, weight_codes, resident_pick):
    length = lax.axis_size("node")
    _, owned, height, width = meson_nodes.shape
    terms = term_nodes.shape[0]
    block = (height, width)
    vmem = pl.BlockSpec(memory_space=pltpu.VMEM)
    smem = pl.BlockSpec(memory_space=pltpu.SMEM)
    dma = pltpu.SemaphoreType.DMA
    slots = owned + FOREIGN
    return pl.pallas_call(
        functools.partial(line_kernel, length, owned, terms),
        out_shape=jax.ShapeDtypeStruct(meson_nodes.shape, jnp.float32),
        in_specs=[pl.BlockSpec(memory_space=pl.ANY), smem, smem, smem],
        out_specs=vmem,
        scratch_shapes=[
            pltpu.VMEM((2, length * owned, 2) + block, jnp.float32),
            pltpu.VMEM((slots, 2) + block, jnp.float32),
            pltpu.VMEM((slots, 2) + block, jnp.float32),
            pltpu.VMEM((2, owned, 2) + block, jnp.float32),
            pltpu.VMEM(((length - 2) * owned, 2) + block, jnp.float32),
            dma((2, owned, 2, PIECES)),
            dma((2, length - 1, owned, 2, PIECES)),
            dma((2, length - 1, owned, 2, PIECES)),
            dma((length, owned, 2, PIECES)),
            dma((length, owned, 2, PIECES)),
            dma((slots, 2, PIECES)),
            dma((slots, 2, PIECES)),
            dma((owned, 2)),
            dma((owned, 2)),
        ],
        compiler_params=pltpu.CompilerParams(
            collective_id=0, has_side_effects=True, vmem_limit_bytes=56 << 20
        ),
    )(meson_nodes, term_nodes.T, weight_codes, resident_pick)


def body(meson_nodes, term_nodes, weight_codes, resident_pick):
    length, owned = lax.axis_size("node"), meson_nodes.shape[1]
    square = meson_nodes.shape[2] == meson_nodes.shape[3]
    halves = lax.axis_size("sub") == 2 and lax.axis_size("rep") == 2
    held = 2 * length * meson_nodes.size * 4
    fits = held <= 16 << 20 and term_nodes.shape[0] <= (length - 2) * owned
    if square and halves and fits and owned == FOREIGN and length == 4:
        return line_body(meson_nodes, term_nodes, weight_codes, resident_pick)
    return wide_body(meson_nodes, term_nodes, weight_codes, resident_pick)


def solution(mesh):
    in_specs = (P(None, ("grp", "node"), "sub", "rep"), P("grp", None), P("grp"), P("grp"))
    out_specs = P(None, ("grp", "node"), "sub", "rep")
    return jax.shard_map(body, mesh=mesh, in_specs=in_specs, out_specs=out_specs, check_vma=False)
```
